32 devices in a mesh: dom: 8 (over z, y), rep: 4 (over x, core).
Axes of the slice: x: 2, y: 2, z: 4, core: 2. Of those that a mesh axis runs over, the one named last changes fastest.
Arguments:
- feats: bfloat16 [256, 32768], P('rep', 'dom'), may hold values from -6 to 6
- w_self: bfloat16 [256, 256], P(None, 'rep'), may hold values from -0.375 to 0.375
- w_neigh: bfloat16 [256, 256], P(None, 'rep'), may hold values from -3 to 3
- local_cols: int32 [256, 2], P('dom'), may hold values from 0 to 31
- local_tiles: bfloat16 [256, 2, 128, 128], P('dom'), may hold values from 0 to 3, as said below
- send_list: int32 [8, 8, 2], P('dom'), may hold values from 0 to 31
- remote_rows: int32 [8, 8, 2], P('dom'), may hold values from 0 to 31
- remote_tiles: bfloat16 [8, 8, 2, 128, 128], P('dom'), may hold values from 0 to 3, as said below
- cotangent: bfloat16 [256, 32768], P('rep', 'dom'), may hold values from -6 to 6
Outputs:
- output: bfloat16 [256, 32768], P('rep', 'dom')
- grad_feats: bfloat16 [256, 32768], P('rep', 'dom')
- grad_w_self: float32 [256, 256], P(None, 'rep')
- grad_w_neigh: float32 [256, 256], P(None, 'rep')
The draws below stay inside these ranges and needn't reach their ends.
Inputs may be any that keep to these rules, and one draw needn't show every extreme that they name: `local_tiles`: edge weights: zero where a tile has no edge, positive otherwise. `remote_tiles`: edge weights: zero where a tile has no edge, positive otherwise.
All inputs are finite; a program needn't handle non-finite values.
Results may differ from the reference program's by a relative error of at most 0.0055.
Values may be sent and summed in bfloat16 or wider, within the bound.
A program may use at most 128 MiB of HBM per device.

```python
import math
import jax
import jax.numpy as jnp
from jax import lax

FEAT = 256
TILE = 128
BLK_DEV = 32
LOC = 2
SLOTS = 2
NODES = 32768
N_DOM = 8


def edge_weights(key, shape, density, low_scale):
    keep_key, value_key, scale_key = jax.random.split(key, 3)
    present = (jax.random.uniform(keep_key, shape, dtype=jnp.float32) < density).astype(jnp.float32)
    values = jax.random.uniform(value_key, shape, dtype=jnp.float32, minval=0.25, maxval=1.0)
    row_shape = tuple(shape[:-1]) + (1,)
    row_scale = jnp.exp(jax.random.uniform(scale_key, row_shape, dtype=jnp.float32, minval=math.log(low_scale), maxval=math.log(3.0)))
    return (present * values * row_scale).astype(jnp.bfloat16)


def draw_local_tiles(key, part):
    shape = (NODES // TILE, LOC, TILE, TILE)
    return edge_weights(jax.random.fold_in(key, 11), shape, 0.2, 0.3)


def draw_remote_tiles(key, part):
    shape = (N_DOM, N_DOM, SLOTS, TILE, TILE)
    return edge_weights(jax.random.fold_in(key, 23), shape, 0.2, 0.3)


def plant(result, own_key, least, largest):
    place = [jax.random.randint(jax.random.fold_in(own_key, axis), (), 0, length) for axis, length in enumerate(result.shape)]
    longest = result.shape.index(max(result.shape))
    next_to = place[:longest] + [(place[longest] + 1) % result.shape[longest]] + place[longest + 1:]
    return result.at[tuple(place)].set(least).at[tuple(next_to)].set(largest)


def level_of(key, shape, cuts, least, top_value):
    loudness = 1.0
    for dim, blocks in cuts:
        heights = jax.random.uniform(jax.random.fold_in(jax.random.fold_in(key, 6), dim), (blocks,), jnp.float32, least / len(cuts), top_value / len(cuts))
        loudness = loudness * jnp.repeat(jnp.exp(heights), shape[dim] // blocks).reshape((-1,) + (1,) * (len(shape) - 1 - dim))
    return loudness


def centred(own_key, shape, width, limit, shards=(), kind=jnp.bfloat16):
    gain = level_of(own_key, shape, shards, -0.22, 0.18) if shards else 1.0
    values = jax.random.normal(own_key, shape, jnp.float32) * width * gain
    return jnp.minimum(jnp.maximum(values, -limit), limit).astype(kind)


def setup_inputs(seed: int = 0) -> dict:
    splits = jax.random.split(jax.random.key(seed), 10)
    feats = centred(splits[0], (FEAT, NODES), 1.0, 6.0, ((0, 4), (1, 8)))
    w_self = centred(splits[1], (FEAT, FEAT), FEAT ** -0.5, 0.375, ((1, 4),))
    w_neigh = centred(splits[2], (FEAT, FEAT), (max(FEAT // 64, 1)) ** -0.5, 3.0, ((1, 4),))
    local_cols = plant(jax.random.randint(splits[3], (NODES // TILE, LOC), 0, BLK_DEV), jax.random.fold_in(splits[3], 1), 0, BLK_DEV - 1).astype(jnp.int32)
    local_tiles = draw_local_tiles(jax.random.fold_in(splits[9], 71), 0)
    send_list = plant(jax.random.randint(splits[5], (N_DOM, N_DOM, SLOTS), 0, BLK_DEV), jax.random.fold_in(splits[5], 1), 0, BLK_DEV - 1).astype(jnp.int32)
    remote_rows = plant(jax.random.randint(splits[6], (N_DOM, N_DOM, SLOTS), 0, BLK_DEV), jax.random.fold_in(splits[6], 1), 0, BLK_DEV - 1).astype(jnp.int32)
    remote_tiles = draw_remote_tiles(jax.random.fold_in(splits[9], 71), 0)
    cotangent = centred(splits[8], (FEAT, NODES), 1.0, 6.0, ((0, 4), (1, 8)))
    return dict(feats=feats, w_self=w_self, w_neigh=w_neigh, local_cols=local_cols, local_tiles=local_tiles, send_list=send_list, remote_rows=remote_rows, remote_tiles=remote_tiles, cotangent=cotangent)


def reference(feats, w_self, w_neigh, local_cols, local_tiles, send_list, remote_rows, remote_tiles, cotangent):
    highest = lax.Precision.HIGHEST
    feat_width, node_count = feats.shape
    block_total = node_count // TILE
    blocked = feats.reshape(feat_width, block_total, TILE)
    block_ids = jnp.arange(BLK_DEV, dtype=jnp.int32)
    local_view = local_tiles.reshape(N_DOM, BLK_DEV, LOC, TILE, TILE)
    col_view = local_cols.reshape(N_DOM, BLK_DEV, LOC)
    sender_base = (jnp.arange(N_DOM, dtype=jnp.int32) * BLK_DEV)[:, None]

    def forward_part(part):
        near_tiles = local_view[part].astype(jnp.float32)
        near_cols = (col_view[part] + part * BLK_DEV).astype(jnp.int32)
        gathered = blocked[:, near_cols].astype(jnp.float32)
        summed = jnp.einsum("fblj,blij->fbi", gathered, near_tiles, precision=highest)
        far_tiles = remote_tiles[part].astype(jnp.float32)
        far_blocks = (sender_base + send_list[:, part, :]).astype(jnp.int32)
        incoming = blocked[:, far_blocks].astype(jnp.float32)
        far_terms = jnp.einsum("fskj,skij->fski", incoming, far_tiles, precision=highest)
        placing = (remote_rows[part][:, :, None] == block_ids).astype(jnp.float32)
        summed = summed + jnp.einsum("fski,skb->fbi", far_terms, placing, precision=highest)
        far_sums = jnp.sum(far_tiles, axis=3)
        divisor = 1.0 + jnp.sum(near_tiles, axis=(1, 3)) + jnp.einsum("ski,skb->bi", far_sums, placing, precision=highest)
        return (summed / divisor).astype(jnp.bfloat16), divisor

    aggregates, divisors = lax.map(forward_part, jnp.arange(N_DOM, dtype=jnp.int32))
    aggregate = aggregates.transpose(1, 0, 2, 3).reshape(feat_width, node_count)
    divisor = divisors.reshape(block_total, TILE)

    preact = jnp.dot(w_self.T, feats, preferred_element_type=jnp.float32)
    preact = preact + jnp.dot(w_neigh.T, aggregate, preferred_element_type=jnp.float32)
    sigmoid_val = jax.nn.sigmoid(preact)
    output = (preact * sigmoid_val).astype(jnp.bfloat16)
    slope = sigmoid_val * (1.0 + preact * (1.0 - sigmoid_val))
    grad_pre = (cotangent.astype(jnp.float32) * slope).astype(jnp.bfloat16)
    grad_w_self = jnp.dot(feats, grad_pre.T, preferred_element_type=jnp.float32)
    grad_w_neigh = jnp.dot(aggregate, grad_pre.T, preferred_element_type=jnp.float32)
    back_self = jnp.dot(w_self, grad_pre, preferred_element_type=jnp.float32)
    back_agg = jnp.dot(w_neigh, grad_pre, preferred_element_type=jnp.float32)
    scaled = (back_agg.reshape(feat_width, block_total, TILE) / divisor).astype(jnp.bfloat16)

    def backward_part(part):
        near_tiles = local_view[part].astype(jnp.float32)
        own_rows = lax.dynamic_slice_in_dim(scaled, (part * BLK_DEV).astype(jnp.int32), BLK_DEV, 1).astype(jnp.float32)
        near_back = jnp.einsum("fbi,blij->fblj", own_rows, near_tiles, precision=highest)
        landing = (col_view[part][:, :, None] == block_ids).astype(jnp.float32)
        collected = jnp.einsum("fblj,blc->fcj", near_back, landing, precision=highest)
        far_rows = (sender_base + remote_rows[:, part, :]).astype(jnp.int32)
        picked = scaled[:, far_rows].astype(jnp.float32)
        far_tiles = remote_tiles[:, part].astype(jnp.float32)
        far_back = jnp.einsum("fdki,dkij->fdkj", picked, far_tiles, precision=highest)
        homing = (send_list[part][:, :, None] == block_ids).astype(jnp.float32)
        return collected + jnp.einsum("fdkj,dkc->fcj", far_back, homing, precision=highest)

    edge_parts = lax.map(backward_part, jnp.arange(N_DOM, dtype=jnp.int32))
    edge_grads = edge_parts.transpose(1, 0, 2, 3).reshape(feat_width, node_count)
    grad_feats = (back_self + edge_grads).astype(jnp.bfloat16)
    return output, grad_feats, grad_w_self, grad_w_neigh
```

```python
import functools

import jax
import jax.numpy as jnp
from jax import lax
from jax.experimental import pallas as pl
from jax.experimental.pallas import tpu as pltpu
from jax.sharding import PartitionSpec as P

MESH = pl.DeviceIdType.MESH
F32 = jnp.float32
BF16 = jnp.bfloat16
CHUNKS = 4
ONES = 16
KEEP = 8
NT = (((1,), (1,)), ((), ()))


def mm(a, b):
    return jnp.dot(a, b, preferred_element_type=F32)


def mm_nt(a, b):
    return lax.dot_general(a, b, NT, preferred_element_type=F32)


def rcopy(src, dst, send, recv, dom, rep):
    return pltpu.make_async_remote_copy(
        src_ref=src,
        dst_ref=dst,
        send_sem=send,
        recv_sem=recv,
        device_id={"dom": dom, "rep": rep},
        device_id_type=MESH,
    )


def greet(devices):
    barrier = pltpu.get_barrier_semaphore()
    for dom, rep in devices:
        pl.semaphore_signal(
            barrier, inc=1, device_id={"dom": dom, "rep": rep}, device_id_type=MESH
        )
    pl.semaphore_wait(barrier, len(devices))


def main_kernel(
    D,
    R,
    feats,
    wts_in,
    wtn_in,
    cols,
    slist,
    place_at,
    ltiles_h,
    rtiles_h,
    cot_h,
    out_o,
    scaled_o,
    bself_o,
    gw_o,
    ltiles,
    rtiles,
    cot,
    blocks_of,
    hsend,
    hrecv,
    summed,
    far,
    inv,
    wts,
    wtn,
    wb,
    xf,
    xa,
    own,
    psend,
    precv,
    gp,
    loc_sem,
    h_s,
    h_r,
    ws_s,
    ws_r,
    wn_s,
    wn_r,
    xf_s,
    xf_r,
    xa_s,
    xa_r,
    pp_s,
    pp_r,
    gx_s,
    gx_r,
    gc_s,
    gc_r,
):
    d, r = lax.axis_index("dom"), lax.axis_index("rep")
    G = R // 2
    c, g = lax.rem(r, 2), lax.div(r, 2)
    mate = g * 2 + 1 - c
    F, N = feats.shape
    B, L, T, _ = ltiles.shape
    K = slist.shape[1]
    CH = N // CHUNKS
    CB = B // CHUNKS

    def cross(q):
        return lax.rem(g + q, G) * 2 + c

    loads = [
        pltpu.make_async_copy(ltiles_h, ltiles, loc_sem.at[0]),
        pltpu.make_async_copy(rtiles_h, rtiles, loc_sem.at[1]),
        pltpu.make_async_copy(cot_h, cot, loc_sem.at[2]),
    ]
    for load in loads:
        load.start()
    for b in range(B):
        blocks_of[b] = feats[:, b * T : (b + 1) * T]
    greet(
        [(lax.rem(d + p, D), r) for p in range(1, D)]
        + [(d, lax.rem(r + j, R)) for j in range(1, R)]
    )

    def halo(p):
        return rcopy(
            hsend.at[p], hrecv.at[p], h_s.at[p], h_r.at[p], lax.rem(d + p, D), r
        )

    def pick(p, dst):
        for k in range(K):
            dst[p, k] = blocks_of[slist[lax.rem(d + p, D), k]]

    def send_halo(p, carry):
        pick(p, hsend)
        halo(p).start()
        return carry

    lax.fori_loop(1, D, send_halo, 0)
    pick(0, hrecv)
    weight_copies = []
    for j in range(1, R):
        to = lax.rem(r + j, R)
        weight_copies.append(
            rcopy(wts_in, wts.at[r], ws_s.at[j], ws_r.at[j], d, to)
        )
        weight_copies.append(
            rcopy(wtn_in, wtn.at[r], wn_s.at[j], wn_r.at[j], d, to)
        )
    for copy in weight_copies:
        copy.start()
    feat_copy = rcopy(feats, xf.at[c], xf_s, xf_r, d, mate)
    feat_copy.start()
    wts[r] = wts_in[...]
    wtn[r] = wtn_in[...]
    xf[c] = feats[...]

    ones = jnp.ones((ONES, T), BF16)
    ones_wide = jnp.ones((ONES, L * T), BF16)
    loads[0].wait()

    def near(b, carry):
        left = jnp.concatenate(
            [
                blocks_of[cols[b, l]]
                for l in range(L)
            ],
            axis=1,
        )
        left = jnp.concatenate([left, ones_wide], axis=0)
        right = jnp.concatenate([ltiles[b, l] for l in range(L)], axis=1)
        summed[b] = mm_nt(left, right)[: F + KEEP]
        return carry

    lax.fori_loop(0, B, near, 0, unroll=4)
    loads[1].wait()

    def far_step(p, carry):
        source = lax.rem(d - p + D, D)
        for k in range(K):
            left = jnp.concatenate([hrecv[p, k], ones], axis=0)
            far[p * K + k] = mm_nt(left, rtiles[source, k])[: F + KEEP]
        return carry

    def far_wait(p, carry):
        halo(p).wait_recv()
        return carry

    far_step(0, 0)
    lax.fori_loop(1, D, far_wait, 0)
    lax.fori_loop(1, D, far_step, 0, unroll=7)

    agg_copies = []
    for ch in range(CHUNKS):

        def place(i, carry):
            b = ch * CB + i
            total = summed[b]

            def add(p, total):
                source = lax.rem(d - p + D, D)
                for k in range(K):
                    hit = place_at[source * K + k, b]
                    total = total + far[p * K + k] * hit
                return total

            total = lax.fori_loop(0, D, add, total, unroll=8)
            inverse = 1.0 / (1.0 + total[F:])
            at = pl.multiple_of(i * T, T)
            whole_at = pl.multiple_of(b * T, T)
            inv[:, pl.ds(whole_at, T)] = inverse
            xa[ch, c, :, pl.ds(at, T)] = (total[:F] * inverse[:1]).astype(BF16)
            return carry

        lax.fori_loop(0, CB, place, 0)
        copy = rcopy(xa.at[ch, c], xa.at[ch, c], xa_s.at[ch], xa_r.at[ch], d, mate)
        copy.start()
        agg_copies.append(copy)

    for copy in weight_copies:
        copy.wait_recv()
    chip = pl.ds(pl.multiple_of(g * 2 * F, 2 * F), 2 * F)
    for i, ref in enumerate((wts, wtn)):
        block = ref[:, :, chip].reshape(R * F, 2 * F)
        turned = block.astype(F32).T.astype(BF16)
        wb[i] = turned.reshape(2, F, R * F)
    lefts = []
    for q in range(G):
        t = cross(q)
        lefts.append(jnp.concatenate([wts[t, :, chip], wtn[t, :, chip]], axis=1))
    left = jnp.concatenate(lefts, axis=0)
    feat_copy.wait_recv()

    def stacked(ch):
        near_part = xf[:, :, ch * CH : (ch + 1) * CH].reshape(2 * F, CH)
        return jnp.concatenate([near_part, xa[ch].reshape(2 * F, CH)], axis=0)

    part_copies = []
    for ch in range(CHUNKS):
        agg_copies[ch].wait_recv()
        part = mm(left, stacked(ch))
        for q in range(1, G):
            psend[q, ch] = part[q * F : (q + 1) * F].astype(BF16)
            copy = rcopy(
                psend.at[q, ch],
                precv.at[q, ch],
                pp_s.at[q, ch],
                pp_r.at[q, ch],
                d,
                cross(q),
            )
            copy.start()
            part_copies.append(copy)
        own[ch] = part[:F]

    loads[2].wait()
    cross_copies, mate_copies = [], []
    for ch in range(CHUNKS):
        preact = own[ch]
        for q in range(1, G):
            part_copies[ch * (G - 1) + q - 1].wait_recv()
            preact = preact + precv[q, ch].astype(F32)
        s = jax.nn.sigmoid(preact)
        at = slice(ch * CH, (ch + 1) * CH)
        out_o[:, at] = (preact * s).astype(BF16)
        slope = s * (1.0 + preact * (1.0 - s))
        gp[ch, r] = (cot[:, at].astype(F32) * slope).astype(BF16)
        for q in range(1, G):
            copy = rcopy(
                gp.at[ch, r],
                gp.at[ch, r],
                gx_s.at[q, ch],
                gx_r.at[q, ch],
                d,
                cross(q),
            )
            copy.start()
            cross_copies.append(copy)
        copy = rcopy(
            gp.at[ch, r], gp.at[ch, r], gc_s.at[0, ch], gc_r.at[0, ch], d, mate
        )
        copy.start()
        mate_copies.append(copy)

    grads = jnp.zeros((G * F, 4 * F), F32)
    for ch in range(CHUNKS):
        blocks = [gp[ch, r]]
        for q in range(1, G):
            cross_copies[ch * (G - 1) + q - 1].wait_recv()
            t = lax.rem(g - q + G, G) * 2 + c
            copy = rcopy(
                gp.at[ch, t], gp.at[ch, t], gc_s.at[q, ch], gc_r.at[q, ch], d, mate
            )
            copy.start()
            mate_copies.append(copy)
        for q in range(1, G):
            blocks.append(gp[ch, cross(q)])
        grads = grads + mm_nt(jnp.concatenate(blocks, axis=0), stacked(ch))
    rows = gw_o.shape[2]
    for p in range(D):
        for q in range(G):
            gw_o[p, q] = grads[q * F + p * rows : q * F + (p + 1) * rows]

    for copy in mate_copies:
        copy.wait_recv()
    back_left = jnp.concatenate([wb[0, c], wb[1, c]], axis=0)
    for ch in range(CHUNKS):
        at = slice(ch * CH, (ch + 1) * CH)
        back = mm(back_left, gp[ch].reshape(R * F, CH))
        bself_o[:, at] = back[:F]
        scaled_o[:, at] = (back[F:] * inv[:1, at]).astype(BF16)

    def drain(p, carry):
        halo(p).wait_send()
        return carry

    lax.fori_loop(1, D, drain, 0)
    for copy in (
        weight_copies
        + [feat_copy]
        + agg_copies
        + part_copies
        + cross_copies
        + mate_copies
    ):
        copy.wait_send()


def scatter_kernel(cols, rrows, scaled, bself, ltiles, rtiles, acc_o, ret_o):
    F, N = scaled.shape
    B, L, T, _ = ltiles.shape
    D, K = rrows.shape
    acc_o[...] = bself[...]

    def near(b, carry):
        left = scaled[:, pl.ds(pl.multiple_of(b * T, T), T)]
        right = jnp.concatenate([ltiles[b, l] for l in range(L)], axis=1)
        back = mm(left, right)
        for l in range(L):
            at = pl.ds(pl.multiple_of(cols[b, l] * T, T), T)
            acc_o[:, at] = acc_o[:, at] + back[:, l * T : (l + 1) * T]
        return carry

    lax.fori_loop(0, B, near, 0, unroll=4)

    def away(s, carry):
        for k in range(K):
            left = scaled[:, pl.ds(pl.multiple_of(rrows[s, k] * T, T), T)]
            ret_o[s, k] = mm(left, rtiles[s, k]).astype(BF16)
        return carry

    lax.fori_loop(0, D, away, 0, unroll=4)


def return_kernel(
    D,
    R,
    home_at,
    acc,
    ret,
    gw,
    gf_o,
    gs_o,
    gn_o,
    back,
    gpart,
    red,
    final,
    h_s,
    h_r,
    p_s,
    p_r,
    f_s,
    f_r,
):
    d, r = lax.axis_index("dom"), lax.axis_index("rep")
    G = R // 2
    c, g = lax.rem(r, 2), lax.div(r, 2)
    F, N = acc.shape
    _, K, _, T = ret.shape
    B = N // T
    rows = gw.shape[2]

    def cross(q):
        return lax.rem(g + q, G) * 2 + c

    greet(
        [
            (lax.rem(d + p, D), cross(q))
            for q in range(G)
            for p in range(D)
            if p or q
        ]
    )
    pieces, halos, finals = [], [], []
    for p in range(1, D):
        to = lax.rem(d + p, D)
        copy = rcopy(gw.at[to], gpart.at[p], p_s.at[p], p_r.at[p], to, r)
        copy.start()
        pieces.append(copy)
    for p in range(1, D):
        to = lax.rem(d + p, D)
        copy = rcopy(ret.at[to], back.at[p], h_s.at[p], h_r.at[p], to, r)
        copy.start()
        halos.append(copy)
    total = gw[d]
    back[0] = ret[d]
    for p in range(1, D):
        pieces[p - 1].wait_recv()
        total = total + gpart[p]
    red[...] = total
    for q in range(G):
        for p in range(D):
            if p or q:
                copy = rcopy(
                    red.at[q],
                    final.at[g, d],
                    f_s.at[q, p],
                    f_r.at[q, p],
                    lax.rem(d + p, D),
                    cross(q),
                )
                copy.start()
                finals.append(copy)
    final[g, d] = red[0]
    for copy in halos:
        copy.wait_recv()

    def home(b, carry):
        at = pl.ds(pl.multiple_of(b * T, T), T)

        def add(p, total):
            source = lax.rem(d - p + D, D)
            for k in range(K):
                hit = home_at[source * K + k, b]
                total = total + back[p, k].astype(F32) * hit
            return total

        total = lax.fori_loop(0, D, add, acc[:, at], unroll=8)
        gf_o[:, at] = total.astype(BF16)
        return carry

    lax.fori_loop(0, B, home, 0)
    for copy in finals:
        copy.wait_recv()
    for h in range(G):
        at = slice(h * 2 * F, (h + 1) * 2 * F)
        for p in range(D):
            piece = final[h, p]
            where = slice(p * rows, (p + 1) * rows)
            gs_o[where, at] = piece[:, : 2 * F]
            gn_o[where, at] = piece[:, 2 * F :]
    for copy in pieces + halos + finals:
        copy.wait_send()


def local(
    D,
    R,
    feats,
    w_self,
    w_neigh,
    local_cols,
    local_tiles,
    send_list,
    remote_rows,
    remote_tiles,
    cotangent,
):
    F, N = feats.shape
    B, L, T, _ = local_tiles.shape
    K = send_list.shape[2]
    G = R // 2
    CH = N // CHUNKS
    rows = F // D
    vmem = pl.BlockSpec(memory_space=pltpu.VMEM)
    smem = pl.BlockSpec(memory_space=pltpu.SMEM)
    hbm = pl.BlockSpec(memory_space=pl.ANY)
    dma = pltpu.SemaphoreType.DMA
    slist, rrows = send_list[0], remote_rows[0]
    far_tiles = remote_tiles[0]
    ids = jnp.arange(B, dtype=jnp.int32)
    place_at = (rrows.reshape(D * K, 1) == ids).astype(F32)
    home_at = (slist.reshape(D * K, 1) == ids).astype(F32)
    limit = 60 * 1024 * 1024
    output, scaled, bself, gw = pl.pallas_call(
        functools.partial(main_kernel, D, R),
        out_shape=(
            jax.ShapeDtypeStruct((F, N), BF16),
            jax.ShapeDtypeStruct((F, N), BF16),
            jax.ShapeDtypeStruct((F, N), F32),
            jax.ShapeDtypeStruct((D, G, rows, 4 * F), F32),
        ),
        in_specs=[vmem, vmem, vmem, smem, smem, smem, hbm, hbm, hbm],
        out_specs=(vmem, vmem, vmem, vmem),
        scratch_shapes=[
            pltpu.VMEM((B, L, T, T), BF16),
            pltpu.VMEM((D, K, T, T), BF16),
            pltpu.VMEM((F, N), BF16),
            pltpu.VMEM((B, F, T), BF16),
            pltpu.VMEM((D, K, F, T), BF16),
            pltpu.VMEM((D, K, F, T), BF16),
            pltpu.VMEM((B, F + KEEP, T), F32),
            pltpu.VMEM((D * K, F + KEEP, T), F32),
            pltpu.VMEM((KEEP, N), F32),
            pltpu.VMEM((R, F, R * F), BF16),
            pltpu.VMEM((R, F, R * F), BF16),
            pltpu.VMEM((2, 2, F, R * F), BF16),
            pltpu.VMEM((2, F, N), BF16),
            pltpu.VMEM((CHUNKS, 2, F, CH), BF16),
            pltpu.VMEM((CHUNKS, F, CH), F32),
            pltpu.VMEM((G, CHUNKS, F, CH), BF16),
            pltpu.VMEM((G, CHUNKS, F, CH), BF16),
            pltpu.VMEM((CHUNKS, R, F, CH), BF16),
            dma((3,)),
            dma((D,)),
            dma((D,)),
            dma((R,)),
            dma((R,)),
            dma((R,)),
            dma((R,)),
            dma,
            dma,
            dma((CHUNKS,)),
            dma((CHUNKS,)),
            dma((G, CHUNKS)),
            dma((G, CHUNKS)),
            dma((G, CHUNKS)),
            dma((G, CHUNKS)),
            dma((G, CHUNKS)),
            dma((G, CHUNKS)),
        ],
        compiler_params=pltpu.CompilerParams(
            collective_id=0, has_side_effects=True, vmem_limit_bytes=limit
        ),
        name="layer_main",
    )(
        feats,
        w_self.T,
        w_neigh.T,
        local_cols,
        slist,
        place_at,
        local_tiles,
        far_tiles,
        cotangent,
    )
    acc, ret = pl.pallas_call(
        scatter_kernel,
        out_shape=(
            jax.ShapeDtypeStruct((F, N), F32),
            jax.ShapeDtypeStruct((D, K, F, T), BF16),
        ),
        in_specs=[smem, smem, vmem, vmem, vmem, vmem],
        out_specs=(vmem, vmem),
        compiler_params=pltpu.CompilerParams(vmem_limit_bytes=limit),
        name="tile_scatter",
    )(local_cols, rrows, scaled, bself, local_tiles, far_tiles)
    grad_feats, gs, gn = pl.pallas_call(
        functools.partial(return_kernel, D, R),
        out_shape=(
            jax.ShapeDtypeStruct((F, N), BF16),
            jax.ShapeDtypeStruct((F, R * F), F32),
            jax.ShapeDtypeStruct((F, R * F), F32),
        ),
        in_specs=[smem, vmem, vmem, vmem],
        out_specs=(vmem, vmem, vmem),
        scratch_shapes=[
            pltpu.VMEM((D, K, F, T), BF16),
            pltpu.VMEM((D, G, rows, 4 * F), F32),
            pltpu.VMEM((G, rows, 4 * F), F32),
            pltpu.VMEM((G, D, rows, 4 * F), F32),
            dma((D,)),
            dma((D,)),
            dma((D,)),
            dma((D,)),
            dma((G, D)),
            dma((G, D)),
        ],
        compiler_params=pltpu.CompilerParams(
            collective_id=1, has_side_effects=True, vmem_limit_bytes=limit
        ),
        name="return_sums",
    )(home_at, acc, ret, gw)
    return output, grad_feats, gs.T, gn.T


def solution(mesh):
    placed = (
        P("rep", "dom"),
        P(None, "rep"),
        P(None, "rep"),
        P("dom", None),
        P("dom", None, None, None),
        P("dom", None, None),
        P("dom", None, None),
        P("dom", None, None, None, None),
        P("rep", "dom"),
    )
    return jax.shard_map(
        functools.partial(local, mesh.shape["dom"], mesh.shape["rep"]),
        mesh=mesh,
        in_specs=placed,
        out_specs=(P("rep", "dom"), P("rep", "dom"), P(None, "rep"), P(None, "rep")),
        check_vma=False,
    )
```

```python
import functools

import jax
import jax.numpy as jnp
from jax import lax
from jax.experimental import pallas as pl
from jax.experimental.pallas import tpu as pltpu
from jax.sharding import PartitionSpec as P

MESH = pl.DeviceIdType.MESH
F32 = jnp.float32
BF16 = jnp.bfloat16
CHUNKS = 4
ONES = 16
KEEP = 8
NT = (((1,), (1,)), ((), ()))


def mm(a, b):
    return jnp.dot(a, b, preferred_element_type=F32)


def mm_nt(a, b):
    return lax.dot_general(a, b, NT, preferred_element_type=F32)


def equal_one(x, y):
    gap = x - y
    return (1 - jnp.minimum(gap * gap, 1)).astype(F32)


def rcopy(src, dst, send, recv, dom, rep):
    return pltpu.make_async_remote_copy(
        src_ref=src,
        dst_ref=dst,
        send_sem=send,
        recv_sem=recv,
        device_id={"dom": dom, "rep": rep},
        device_id_type=MESH,
    )


def greet(devices):
    barrier = pltpu.get_barrier_semaphore()
    for dom, rep in devices:
        pl.semaphore_signal(
            barrier, inc=1, device_id={"dom": dom, "rep": rep}, device_id_type=MESH
        )
    pl.semaphore_wait(barrier, len(devices))


def main_kernel(
    D,
    R,
    feats,
    wts_in,
    wtn_in,
    cols,
    slist,
    rrows,
    ltiles_h,
    rtiles_h,
    cot_h,
    out_o,
    acc_o,
    back_o,
    final_o,
    ltiles,
    rtiles,
    cot,
    blocks_of,
    hsend,
    hrecv,
    summed,
    far,
    inv,
    wts,
    wtn,
    wb,
    xf,
    xa,
    own,
    psend,
    precv,
    gp,
    gw,
    gpart,
    red,
    scaled,
    ret,
    nearb,
    loc_sem,
    h_s,
    h_r,
    ws_s,
    ws_r,
    wn_s,
    wn_r,
    xf_s,
    xf_r,
    xa_s,
    xa_r,
    pp_s,
    pp_r,
    gx_s,
    gx_r,
    gc_s,
    gc_r,
    b_s,
    b_r,
    p_s,
    p_r,
    f_s,
    f_r,
):
    d, r = lax.axis_index("dom"), lax.axis_index("rep")
    G = R // 2
    c, g = lax.rem(r, 2), lax.div(r, 2)
    mate = g * 2 + 1 - c
    F, N = feats.shape
    B, L, T, _ = ltiles.shape
    K = slist.shape[0]
    CH = N // CHUNKS
    CB = B // CHUNKS

    def cross(q):
        return lax.rem(g + q, G) * 2 + c

    loads = [
        pltpu.make_async_copy(ltiles_h, ltiles, loc_sem.at[0]),
        pltpu.make_async_copy(rtiles_h, rtiles, loc_sem.at[1]),
        pltpu.make_async_copy(cot_h, cot, loc_sem.at[2]),
    ]
    for load in loads:
        load.start()
    for b in range(B):
        blocks_of[b] = feats[:, b * T : (b + 1) * T]
    greet(
        [
            (lax.rem(d + p, D), cross(q))
            for q in range(G)
            for p in range(D)
            if p or q
        ]
        + [(d, lax.rem(g + q, G) * 2 + 1 - c) for q in range(G)]
    )

    def halo(p):
        return rcopy(
            hsend.at[p], hrecv.at[p], h_s.at[p], h_r.at[p], lax.rem(d + p, D), r
        )

    def pick(p, dst):
        for k in range(K):
            dst[p, k] = blocks_of[slist[k, lax.rem(d + p, D)]]

    def send_halo(p, carry):
        pick(p, hsend)
        halo(p).start()
        return carry

    lax.fori_loop(1, D, send_halo, 0)
    pick(0, hrecv)
    weight_copies = []
    for j in range(1, R):
        to = lax.rem(r + j, R)
        weight_copies.append(
            rcopy(wts_in, wts.at[r], ws_s.at[j], ws_r.at[j], d, to)
        )
        weight_copies.append(
            rcopy(wtn_in, wtn.at[r], wn_s.at[j], wn_r.at[j], d, to)
        )
    for copy in weight_copies:
        copy.start()
    feat_copy = rcopy(feats, xf.at[c], xf_s, xf_r, d, mate)
    feat_copy.start()
    wts[r] = wts_in[...]
    wtn[r] = wtn_in[...]
    xf[c] = feats[...]

    ones = jnp.ones((ONES, T), BF16)
    ones_wide = jnp.ones((ONES, L * T), BF16)
    loads[0].wait()

    def near(b, carry):
        left = jnp.concatenate(
            [
                blocks_of[cols[l, b]]
                for l in range(L)
            ],
            axis=1,
        )
        left = jnp.concatenate([left, ones_wide], axis=0)
        right = jnp.concatenate([ltiles[b, l] for l in range(L)], axis=1)
        summed[b] = mm_nt(left, right)[: F + KEEP]
        return carry

    lax.fori_loop(0, B, near, 0, unroll=4)
    loads[1].wait()

    def far_step(p, carry):
        source = lax.rem(d - p + D, D)
        for k in range(K):
            left = jnp.concatenate([hrecv[p, k], ones], axis=0)
            far[p * K + k] = mm_nt(left, rtiles[source, k])[: F + KEEP]
        return carry

    def far_wait(p, carry):
        halo(p).wait_recv()
        return carry

    far_step(0, 0)
    lax.fori_loop(1, D, far_wait, 0)
    lax.fori_loop(1, D, far_step, 0, unroll=7)

    agg_copies = []
    for ch in range(CHUNKS):

        def place(i, carry):
            b = ch * CB + i
            total = summed[b]

            def add(p, total):
                source = lax.rem(d - p + D, D)
                for k in range(K):
                    hit = equal_one(rrows[k, source], b)
                    total = total + far[p * K + k] * hit
                return total

            total = lax.fori_loop(0, D, add, total, unroll=8)
            inverse = 1.0 / (1.0 + total[F:])
            at = pl.multiple_of(i * T, T)
            whole_at = pl.multiple_of(b * T, T)
            inv[:, pl.ds(whole_at, T)] = inverse
            xa[ch, c, :, pl.ds(at, T)] = (total[:F] * inverse[:1]).astype(BF16)
            return carry

        lax.fori_loop(0, CB, place, 0)
        copy = rcopy(xa.at[ch, c], xa.at[ch, c], xa_s.at[ch], xa_r.at[ch], d, mate)
        copy.start()
        agg_copies.append(copy)

    for copy in weight_copies:
        copy.wait_recv()
    chip = pl.ds(pl.multiple_of(g * 2 * F, 2 * F), 2 * F)
    for i, ref in enumerate((wts, wtn)):
        block = ref[:, :, chip].reshape(R * F, 2 * F)
        turned = block.astype(F32).T.astype(BF16)
        wb[i] = turned.reshape(2, F, R * F)
    lefts = []
    for q in range(G):
        t = cross(q)
        lefts.append(jnp.concatenate([wts[t, :, chip], wtn[t, :, chip]], axis=1))
    left = jnp.concatenate(lefts, axis=0)
    feat_copy.wait_recv()

    def stacked(ch):
        near_part = xf[:, :, ch * CH : (ch + 1) * CH].reshape(2 * F, CH)
        return jnp.concatenate([near_part, xa[ch].reshape(2 * F, CH)], axis=0)

    part_copies = []
    for ch in range(CHUNKS):
        agg_copies[ch].wait_recv()
        part = mm(left, stacked(ch))
        for q in range(1, G):
            psend[q, ch] = part[q * F : (q + 1) * F].astype(BF16)
            copy = rcopy(
                psend.at[q, ch],
                precv.at[q, ch],
                pp_s.at[q, ch],
                pp_r.at[q, ch],
                d,
                cross(q),
            )
            copy.start()
            part_copies.append(copy)
        own[ch] = part[:F]

    loads[2].wait()
    cross_copies, mate_copies = [], []
    for ch in range(CHUNKS):
        preact = own[ch]
        for q in range(1, G):
            part_copies[ch * (G - 1) + q - 1].wait_recv()
            preact = preact + precv[q, ch].astype(F32)
        s = jax.nn.sigmoid(preact)
        at = slice(ch * CH, (ch + 1) * CH)
        out_o[:, at] = (preact * s).astype(BF16)
        slope = s * (1.0 + preact * (1.0 - s))
        gp[ch, r] = (cot[:, at].astype(F32) * slope).astype(BF16)
        for q in range(1, G):
            copy = rcopy(
                gp.at[ch, r],
                gp.at[ch, r],
                gx_s.at[q, ch],
                gx_r.at[q, ch],
                d,
                cross(q),
            )
            copy.start()
            cross_copies.append(copy)
        copy = rcopy(
            gp.at[ch, r], gp.at[ch, r], gc_s.at[0, ch], gc_r.at[0, ch], d, mate
        )
        copy.start()
        mate_copies.append(copy)

    grads = jnp.zeros((G * F, 4 * F), F32)
    for ch in range(CHUNKS):
        blocks = [gp[ch, r]]
        for q in range(1, G):
            cross_copies[ch * (G - 1) + q - 1].wait_recv()
            t = lax.rem(g - q + G, G) * 2 + c
            copy = rcopy(
                gp.at[ch, t], gp.at[ch, t], gc_s.at[q, ch], gc_r.at[q, ch], d, mate
            )
            copy.start()
            mate_copies.append(copy)
        for q in range(1, G):
            blocks.append(gp[ch, cross(q)])
        grads = grads + mm_nt(jnp.concatenate(blocks, axis=0), stacked(ch))
    rows = gw.shape[2]
    for p in range(D):
        for q in range(G):
            gw[p, q] = grads[q * F + p * rows : q * F + (p + 1) * rows]

    def piece(p):
        to = lax.rem(d + p, D)
        return rcopy(gw.at[to], gpart.at[p], p_s.at[p], p_r.at[p], to, r)

    def send_piece(p, carry):
        piece(p).start()
        return carry

    lax.fori_loop(1, D, send_piece, 0)

    back_left = jnp.concatenate([wb[0, c], wb[1, c]], axis=0)
    for ch in range(CHUNKS):
        later = CHUNKS + ch * (G - 1)
        for copy in [mate_copies[ch]] + mate_copies[later : later + G - 1]:
            copy.wait_recv()
        back = mm(back_left, gp[ch].reshape(R * F, CH))
        for i in range(CB):
            b = ch * CB + i
            at = slice(i * T, (i + 1) * T)
            whole_at = slice(b * T, (b + 1) * T)
            acc_o[:, whole_at] = back[:F, at]
            scaled[b] = (back[F:, at] * inv[:1, whole_at]).astype(BF16)

    def away(p, dst, slot):
        source = lax.rem(d + p, D)
        for k in range(K):
            block = scaled[rrows[k, source]]
            dst[slot, k] = mm(block, rtiles[source, k]).astype(BF16)

    def returned(p):
        to = lax.rem(d + p, D)
        return rcopy(ret.at[p], back_o.at[d], b_s.at[p], b_r.at[p], to, r)

    def send_back(p, carry):
        away(p, ret, p)
        returned(p).start()
        return carry

    lax.fori_loop(1, D, send_back, 0, unroll=7)
    away(0, back_o, d)

    def take_piece(p, total):
        piece(p).wait_recv()
        return total + gpart[p]

    red[...] = lax.fori_loop(1, D, take_piece, gw[d])
    finals = []
    for q in range(G):
        for p in range(D):
            if p or q:
                copy = rcopy(
                    red.at[q],
                    final_o.at[g, d],
                    f_s.at[q, p],
                    f_r.at[q, p],
                    lax.rem(d + p, D),
                    cross(q),
                )
                copy.start()
                finals.append(copy)
    final_o[g, d] = red[0]

    def near_back(b, carry):
        right = jnp.concatenate([ltiles[b, l] for l in range(L)], axis=1)
        both = mm(scaled[b], right)
        for l in range(L):
            nearb[l, b] = both[:, l * T : (l + 1) * T]
        return carry

    lax.fori_loop(0, B, near_back, 0, unroll=4)

    def gather_back(block, carry):
        at = pl.ds(pl.multiple_of(block * T, T), T)

        def add(b, total):
            for l in range(L):
                total = total + nearb[l, b] * equal_one(cols[l, b], block)
            return total

        acc_o[:, at] = lax.fori_loop(0, B, add, acc_o[:, at], unroll=8)
        return carry

    lax.fori_loop(0, B, gather_back, 0)

    def finish_back(p, carry):
        returned(p).wait()
        piece(p).wait_send()
        return carry

    lax.fori_loop(1, D, finish_back, 0)
    for copy in finals:
        copy.wait_recv()

    def drain(p, carry):
        halo(p).wait_send()
        return carry

    lax.fori_loop(1, D, drain, 0)
    for copy in (
        weight_copies
        + [feat_copy]
        + agg_copies
        + part_copies
        + cross_copies
        + mate_copies
        + finals
    ):
        copy.wait_send()


def finish_kernel(slist, acc, back, final, out, out_o, gf_o, gs_o, gn_o, total):
    F, N = acc.shape
    D, K, _, T = back.shape
    G, _, rows, width = final.shape
    half = width // 2
    out_o[...] = out[...]
    total[...] = acc[...]

    def home(s, carry):
        for k in range(K):
            at = pl.ds(pl.multiple_of(slist[k, s] * T, T), T)
            total[:, at] = total[:, at] + back[s, k].astype(F32)
        return carry

    lax.fori_loop(0, D, home, 0)
    gf_o[...] = total[...].astype(BF16)
    for h in range(G):
        at = slice(h * half, (h + 1) * half)
        for p in range(D):
            part = final[h, p]
            where = slice(p * rows, (p + 1) * rows)
            gs_o[where, at] = part[:, :half]
            gn_o[where, at] = part[:, half:]


def local(
    D,
    R,
    feats,
    w_self,
    w_neigh,
    local_cols,
    local_tiles,
    send_list,
    remote_rows,
    remote_tiles,
    cotangent,
):
    F, N = feats.shape
    B, L, T, _ = local_tiles.shape
    K = send_list.shape[2]
    G = R // 2
    CH = N // CHUNKS
    rows = F // D
    vmem = pl.BlockSpec(memory_space=pltpu.VMEM)
    smem = pl.BlockSpec(memory_space=pltpu.SMEM)
    hbm = pl.BlockSpec(memory_space=pl.ANY)
    dma = pltpu.SemaphoreType.DMA
    slist = jnp.swapaxes(send_list, 1, 2)[0]
    rrows = jnp.swapaxes(remote_rows, 1, 2)[0]
    far_tiles = remote_tiles[0]
    limit = 60 * 1024 * 1024
    output, acc, back, final = pl.pallas_call(
        functools.partial(main_kernel, D, R),
        out_shape=(
            jax.ShapeDtypeStruct((F, N), BF16),
            jax.ShapeDtypeStruct((F, N), F32),
            jax.ShapeDtypeStruct((D, K, F, T), BF16),
            jax.ShapeDtypeStruct((G, D, rows, 4 * F), F32),
        ),
        in_specs=[vmem, vmem, vmem, smem, smem, smem, hbm, hbm, hbm],
        out_specs=(vmem, vmem, vmem, vmem),
        scratch_shapes=[
            pltpu.VMEM((B, L, T, T), BF16),
            pltpu.VMEM((D, K, T, T), BF16),
            pltpu.VMEM((F, N), BF16),
            pltpu.VMEM((B, F, T), BF16),
            pltpu.VMEM((D, K, F, T), BF16),
            pltpu.VMEM((D, K, F, T), BF16),
            pltpu.VMEM((B, F + KEEP, T), F32),
            pltpu.VMEM((D * K, F + KEEP, T), F32),
            pltpu.VMEM((KEEP, N), F32),
            pltpu.VMEM((R, F, R * F), BF16),
            pltpu.VMEM((R, F, R * F), BF16),
            pltpu.VMEM((2, 2, F, R * F), BF16),
            pltpu.VMEM((2, F, N), BF16),
            pltpu.VMEM((CHUNKS, 2, F, CH), BF16),
            pltpu.VMEM((CHUNKS, F, CH), F32),
            pltpu.VMEM((G, CHUNKS, F, CH), BF16),
            pltpu.VMEM((G, CHUNKS, F, CH), BF16),
            pltpu.VMEM((CHUNKS, R, F, CH), BF16),
            pltpu.VMEM((D, G, rows, 4 * F), F32),
            pltpu.VMEM((D, G, rows, 4 * F), F32),
            pltpu.VMEM((G, rows, 4 * F), F32),
            pltpu.VMEM((B, F, T), BF16),
            pltpu.VMEM((D, K, F, T), BF16),
            pltpu.VMEM((L, B, F, T), F32),
            dma((3,)),
            dma((D,)),
            dma((D,)),
            dma((R,)),
            dma((R,)),
            dma((R,)),
            dma((R,)),
            dma,
            dma,
            dma((CHUNKS,)),
            dma((CHUNKS,)),
            dma((G, CHUNKS)),
            dma((G, CHUNKS)),
            dma((G, CHUNKS)),
            dma((G, CHUNKS)),
            dma((G, CHUNKS)),
            dma((G, CHUNKS)),
            dma((D,)),
            dma((D,)),
            dma((D,)),
            dma((D,)),
            dma((G, D)),
            dma((G, D)),
        ],
        compiler_params=pltpu.CompilerParams(
            collective_id=0, has_side_effects=True, vmem_limit_bytes=limit
        ),
        name="layer_main",
    )(
        feats,
        w_self.T,
        w_neigh.T,
        local_cols.T,
        slist,
        rrows,
        local_tiles,
        far_tiles,
        cotangent,
    )
    output, grad_feats, gs, gn = pl.pallas_call(
        finish_kernel,
        out_shape=(
            jax.ShapeDtypeStruct((F, N), BF16),
            jax.ShapeDtypeStruct((F, N), BF16),
            jax.ShapeDtypeStruct((F, R * F), F32),
            jax.ShapeDtypeStruct((F, R * F), F32),
        ),
        in_specs=[smem, vmem, vmem, vmem, vmem],
        out_specs=(vmem, vmem, vmem, vmem),
        scratch_shapes=[pltpu.VMEM((F, N), F32)],
        compiler_params=pltpu.CompilerParams(vmem_limit_bytes=limit // 4),
        name="finish",
    )(slist, acc, back, final, output)
    return output, grad_feats, gs.T, gn.T


def solution(mesh):
    placed = (
        P("rep", "dom"),
        P(None, "rep"),
        P(None, "rep"),
        P("dom", None),
        P("dom", None, None, None),
        P("dom", None, None),
        P("dom", None, None),
        P("dom", None, None, None, None),
        P("rep", "dom"),
    )
    return jax.shard_map(
        functools.partial(local, mesh.shape["dom"], mesh.shape["rep"]),
        mesh=mesh,
        in_specs=placed,
        out_specs=(P("rep", "dom"), P("rep", "dom"), P(None, "rep"), P(None, "rep")),
        check_vma=False,
    )
```

```python
import functools

import jax
import jax.numpy as jnp
from jax import lax
from jax.experimental import pallas as pl
from jax.experimental.pallas import tpu as pltpu
from jax.sharding import PartitionSpec as P

MESH = pl.DeviceIdType.MESH
F32 = jnp.float32
BF16 = jnp.bfloat16
CHUNKS = 4
ONES = 16
KEEP = 8
NT = (((1,), (1,)), ((), ()))


def mm(a, b):
    return jnp.dot(a, b, preferred_element_type=F32)


def mm_nt(a, b):
    return lax.dot_general(a, b, NT, preferred_element_type=F32)


def equal_one(x, y):
    gap = x - y
    return (1 - jnp.minimum(gap * gap, 1)).astype(F32)


def rcopy(src, dst, send, recv, dom, rep):
    return pltpu.make_async_remote_copy(
        src_ref=src,
        dst_ref=dst,
        send_sem=send,
        recv_sem=recv,
        device_id={"dom": dom, "rep": rep},
        device_id_type=MESH,
    )


def greet(devices):
    barrier = pltpu.get_barrier_semaphore()
    for dom, rep in devices:
        pl.semaphore_signal(
            barrier, inc=1, device_id={"dom": dom, "rep": rep}, device_id_type=MESH
        )
    pl.semaphore_wait(barrier, len(devices))


def main_kernel(
    D,
    R,
    feats,
    wts_in,
    wtn_in,
    cols,
    slist,
    rrows,
    ltiles_h,
    rtiles_h,
    cot_h,
    out_o,
    acc_o,
    back_o,
    final_o,
    ltiles,
    rtiles,
    cot,
    blocks_of,
    hsend,
    hrecv,
    summed,
    far,
    inv,
    wts,
    wtn,
    wb,
    xf,
    xa,
    own,
    psend,
    precv,
    gp,
    gw,
    gpart,
    red,
    scaled,
    ret,
    nearb,
    loc_sem,
    h_s,
    h_r,
    ws_s,
    ws_r,
    wn_s,
    wn_r,
    xf_s,
    xf_r,
    xa_s,
    xa_r,
    pp_s,
    pp_r,
    gx_s,
    gx_r,
    gc_s,
    gc_r,
    b_s,
    b_r,
    p_s,
    p_r,
    f_s,
    f_r,
):
    d, r = lax.axis_index("dom"), lax.axis_index("rep")
    G = R // 2
    c, g = lax.rem(r, 2), lax.div(r, 2)
    mate = g * 2 + 1 - c
    F, N = feats.shape
    B, L, T, _ = ltiles.shape
    K = slist.shape[0]
    CH = N // CHUNKS
    CB = B // CHUNKS

    def cross(q):
        return lax.rem(g + q, G) * 2 + c

    loads = [
        pltpu.make_async_copy(ltiles_h, ltiles, loc_sem.at[0]),
        pltpu.make_async_copy(rtiles_h, rtiles, loc_sem.at[1]),
        pltpu.make_async_copy(cot_h, cot, loc_sem.at[2]),
    ]
    for load in loads:
        load.start()
    for b in range(B):
        blocks_of[b] = feats[:, b * T : (b + 1) * T]
    greet(
        [
            (lax.rem(d + p, D), cross(q))
            for q in range(G)
            for p in range(D)
            if p or q
        ]
        + [(d, lax.rem(g + q, G) * 2 + 1 - c) for q in range(G)]
    )

    def halo(p):
        return rcopy(
            hsend.at[p], hrecv.at[p], h_s.at[p], h_r.at[p], lax.rem(d + p, D), r
        )

    def pick(p, dst):
        for k in range(K):
            dst[p, k] = blocks_of[slist[k, lax.rem(d + p, D)]]

    def send_halo(p, carry):
        pick(p, hsend)
        halo(p).start()
        return carry

    lax.fori_loop(1, D, send_halo, 0)
    pick(0, hrecv)
    weight_copies, cross_weights = [], []
    sets = ((wts_in, wts, ws_s, ws_r), (wtn_in, wtn, wn_s, wn_r))
    chip = pl.ds(pl.multiple_of(g * 2 * F, 2 * F), 2 * F)
    for q in range(1, G):
        there = lax.rem(g + q, G)
        cut = pl.ds(pl.multiple_of(there * 2 * F, 2 * F), 2 * F)
        for src, dst, ss, rs in sets:
            cross_weights.append(
                rcopy(src.at[:, cut], dst.at[r], ss.at[q], rs.at[q], d, cross(q))
            )
    for src, dst, ss, rs in sets:
        weight_copies.append(
            rcopy(src.at[:, chip], dst.at[r], ss.at[0], rs.at[0], d, mate)
        )
    for copy in cross_weights + weight_copies:
        copy.start()
    feat_copy = rcopy(feats, xf.at[c], xf_s, xf_r, d, mate)
    feat_copy.start()
    wts[r] = wts_in[:, chip]
    wtn[r] = wtn_in[:, chip]
    acc_o[...] = jnp.zeros((F, N), F32)
    xf[c] = feats[...]

    ones = jnp.ones((ONES, T), BF16)
    ones_wide = jnp.ones((ONES, L * T), BF16)
    loads[0].wait()

    def near(b, carry):
        left = jnp.concatenate(
            [
                blocks_of[cols[l, b]]
                for l in range(L)
            ],
            axis=1,
        )
        left = jnp.concatenate([left, ones_wide], axis=0)
        right = jnp.concatenate([ltiles[b, l] for l in range(L)], axis=1)
        summed[b] = mm_nt(left, right)[: F + KEEP]
        return carry

    lax.fori_loop(0, B, near, 0, unroll=4)
    for copy in cross_weights:
        copy.wait_recv()
    for q in range(1, G):
        t = lax.rem(g - q + G, G) * 2 + c
        for _, dst, ss, rs in sets:
            slot = G + q - 1
            copy = rcopy(dst.at[t], dst.at[t], ss.at[slot], rs.at[slot], d, mate)
            copy.start()
            weight_copies.append(copy)
    loads[1].wait()

    def far_step(p, carry):
        source = lax.rem(d - p + D, D)
        for k in range(K):
            left = jnp.concatenate([hrecv[p, k], ones], axis=0)
            far[p * K + k] = mm_nt(left, rtiles[source, k])[: F + KEEP]
        return carry

    def far_wait(p, carry):
        halo(p).wait_recv()
        return carry

    far_step(0, 0)
    lax.fori_loop(1, D, far_wait, 0)
    lax.fori_loop(1, D, far_step, 0, unroll=7)

    agg_copies = []
    for ch in range(CHUNKS):

        def place(i, carry):
            b = ch * CB + i
            total = summed[b]

            def add(p, total):
                source = lax.rem(d - p + D, D)
                for k in range(K):
                    hit = equal_one(rrows[k, source], b)
                    total = total + far[p * K + k] * hit
                return total

            total = lax.fori_loop(0, D, add, total, unroll=8)
            inverse = 1.0 / (1.0 + total[F:])
            at = pl.multiple_of(i * T, T)
            whole_at = pl.multiple_of(b * T, T)
            inv[:, pl.ds(whole_at, T)] = inverse
            xa[ch, c, :, pl.ds(at, T)] = (total[:F] * inverse[:1]).astype(BF16)
            return carry

        lax.fori_loop(0, CB, place, 0)
        copy = rcopy(xa.at[ch, c], xa.at[ch, c], xa_s.at[ch], xa_r.at[ch], d, mate)
        copy.start()
        agg_copies.append(copy)

    for copy in weight_copies:
        copy.wait_recv()
    for i, ref in enumerate((wts, wtn)):
        block = ref[...].reshape(R * F, 2 * F)
        turned = block.astype(F32).T.astype(BF16)
        wb[i] = turned.reshape(2, F, R * F)
    lefts = []
    for q in range(G):
        t = cross(q)
        lefts.append(jnp.concatenate([wts[t], wtn[t]], axis=1))
    left = jnp.concatenate(lefts, axis=0)
    feat_copy.wait_recv()

    def stacked(ch):
        near_part = xf[:, :, ch * CH : (ch + 1) * CH].reshape(2 * F, CH)
        return jnp.concatenate([near_part, xa[ch].reshape(2 * F, CH)], axis=0)

    part_copies = []
    for ch in range(CHUNKS):
        agg_copies[ch].wait_recv()
        part = mm(left, stacked(ch))
        for q in range(1, G):
            psend[q, ch] = part[q * F : (q + 1) * F].astype(BF16)
            copy = rcopy(
                psend.at[q, ch],
                precv.at[q, ch],
                pp_s.at[q, ch],
                pp_r.at[q, ch],
                d,
                cross(q),
            )
            copy.start()
            part_copies.append(copy)
        own[ch] = part[:F]

    loads[2].wait()
    cross_copies, mate_copies = [], []
    for ch in range(CHUNKS):
        preact = own[ch]
        for q in range(1, G):
            part_copies[ch * (G - 1) + q - 1].wait_recv()
            preact = preact + precv[q, ch].astype(F32)
        s = jax.nn.sigmoid(preact)
        at = slice(ch * CH, (ch + 1) * CH)
        out_o[:, at] = (preact * s).astype(BF16)
        slope = s * (1.0 + preact * (1.0 - s))
        gp[ch, r] = (cot[:, at].astype(F32) * slope).astype(BF16)
        for q in range(1, G):
            copy = rcopy(
                gp.at[ch, r],
                gp.at[ch, r],
                gx_s.at[q, ch],
                gx_r.at[q, ch],
                d,
                cross(q),
            )
            copy.start()
            cross_copies.append(copy)
        copy = rcopy(
            gp.at[ch, r], gp.at[ch, r], gc_s.at[0, ch], gc_r.at[0, ch], d, mate
        )
        copy.start()
        mate_copies.append(copy)

    back_left = jnp.concatenate([wb[0, c], wb[1, c]], axis=0)

    def back_chunk(ch):
        later = CHUNKS + ch * (G - 1)
        for copy in [mate_copies[ch]] + mate_copies[later : later + G - 1]:
            copy.wait_recv()
        back = mm(back_left, gp[ch].reshape(R * F, CH))
        for i in range(CB):
            b = ch * CB + i
            at = slice(i * T, (i + 1) * T)
            whole_at = slice(b * T, (b + 1) * T)
            acc_o[:, whole_at] += back[:F, at]
            scaled[b] = (back[F:, at] * inv[:1, whole_at]).astype(BF16)

    def scatter_chunk(ch):
        first = ch * CB

        def near_back(i, carry):
            b = first + i
            right = jnp.concatenate([ltiles[b, l] for l in range(L)], axis=1)
            both = mm(scaled[b], right)
            for l in range(L):
                nearb[l, i] = both[:, l * T : (l + 1) * T]
            return carry

        lax.fori_loop(0, CB, near_back, 0, unroll=4)

        def gather_back(block, carry):
            at = pl.ds(pl.multiple_of(block * T, T), T)

            def add(i, total):
                for l in range(L):
                    total = total + nearb[l, i] * equal_one(cols[l, first + i], block)
                return total

            acc_o[:, at] = lax.fori_loop(0, CB, add, acc_o[:, at], unroll=8)
            return carry

        lax.fori_loop(0, B, gather_back, 0)

    grads = jnp.zeros((G * F, 4 * F), F32)
    for ch in range(CHUNKS):
        blocks = [gp[ch, r]]
        for q in range(1, G):
            cross_copies[ch * (G - 1) + q - 1].wait_recv()
            t = lax.rem(g - q + G, G) * 2 + c
            copy = rcopy(
                gp.at[ch, t], gp.at[ch, t], gc_s.at[q, ch], gc_r.at[q, ch], d, mate
            )
            copy.start()
            mate_copies.append(copy)
        for q in range(1, G):
            blocks.append(gp[ch, cross(q)])
        grads = grads + mm_nt(jnp.concatenate(blocks, axis=0), stacked(ch))
        if ch >= 1:
            back_chunk(ch - 1)
        if ch >= 1 and ch + 1 < CHUNKS:
            scatter_chunk(ch - 1)
    rows = gw.shape[2]
    for p in range(D):
        for q in range(G):
            gw[p, q] = grads[q * F + p * rows : q * F + (p + 1) * rows]

    def piece(p):
        to = lax.rem(d + p, D)
        return rcopy(gw.at[to], gpart.at[p], p_s.at[p], p_r.at[p], to, r)

    def send_piece(p, carry):
        piece(p).start()
        return carry

    lax.fori_loop(1, D, send_piece, 0)

    back_chunk(CHUNKS - 1)

    def away(p, dst, slot):
        source = lax.rem(d + p, D)
        for k in range(K):
            block = scaled[rrows[k, source]]
            dst[slot, k] = mm(block, rtiles[source, k]).astype(BF16)

    def returned(p):
        to = lax.rem(d + p, D)
        return rcopy(ret.at[p], back_o.at[d], b_s.at[p], b_r.at[p], to, r)

    def send_back(p, carry):
        away(p, ret, p)
        returned(p).start()
        return carry

    lax.fori_loop(1, D, send_back, 0, unroll=7)
    away(0, back_o, d)

    def take_piece(p, total):
        piece(p).wait_recv()
        return total + gpart[p]

    red[...] = lax.fori_loop(1, D, take_piece, gw[d])
    finals = []
    for q in range(G):
        for p in range(D):
            if p or q:
                copy = rcopy(
                    red.at[q],
                    final_o.at[g, d],
                    f_s.at[q, p],
                    f_r.at[q, p],
                    lax.rem(d + p, D),
                    cross(q),
                )
                copy.start()
                finals.append(copy)
    final_o[g, d] = red[0]

    for ch in range(max(CHUNKS - 2, 0), CHUNKS):
        scatter_chunk(ch)

    def finish_back(p, carry):
        returned(p).wait()
        piece(p).wait_send()
        return carry

    lax.fori_loop(1, D, finish_back, 0)
    for copy in finals:
        copy.wait_recv()

    def drain(p, carry):
        halo(p).wait_send()
        return carry

    lax.fori_loop(1, D, drain, 0)
    for copy in (
        weight_copies
        + cross_weights
        + [feat_copy]
        + agg_copies
        + part_copies
        + cross_copies
        + mate_copies
        + finals
    ):
        copy.wait_send()


def finish_kernel(
    slist, acc_h, back_h, final_h, out_h, out_o, gf_o, gs_o, gn_o, total, back, final, sem
):
    F, N = acc_h.shape
    loads = [
        pltpu.make_async_copy(src, dst, sem.at[i])
        for i, (src, dst) in enumerate(
            ((out_h, out_o), (acc_h, total), (back_h, back), (final_h, final))
        )
    ]
    for load in loads:
        load.start()
    D, K, _, T = back.shape
    G, _, rows, width = final.shape
    half = width // 2
    for load in loads[1:]:
        load.wait()

    def home(s, carry):
        for k in range(K):
            at = pl.ds(pl.multiple_of(slist[k, s] * T, T), T)
            total[:, at] = total[:, at] + back[s, k].astype(F32)
        return carry

    lax.fori_loop(0, D, home, 0)
    gf_o[...] = total[...].astype(BF16)
    for h in range(G):
        at = slice(h * half, (h + 1) * half)
        for p in range(D):
            part = final[h, p]
            where = slice(p * rows, (p + 1) * rows)
            gs_o[where, at] = part[:, :half]
            gn_o[where, at] = part[:, half:]
    loads[0].wait()


def local(
    D,
    R,
    feats,
    w_self,
    w_neigh,
    local_cols,
    local_tiles,
    send_list,
    remote_rows,
    remote_tiles,
    cotangent,
):
    F, N = feats.shape
    B, L, T, _ = local_tiles.shape
    K = send_list.shape[2]
    G = R // 2
    CH = N // CHUNKS
    rows = F // D
    vmem = pl.BlockSpec(memory_space=pltpu.VMEM)
    smem = pl.BlockSpec(memory_space=pltpu.SMEM)
    hbm = pl.BlockSpec(memory_space=pl.ANY)
    dma = pltpu.SemaphoreType.DMA
    slist = jnp.swapaxes(send_list, 1, 2)[0]
    rrows = jnp.swapaxes(remote_rows, 1, 2)[0]
    far_tiles = remote_tiles[0]
    limit = 60 * 1024 * 1024
    output, acc, back, final = pl.pallas_call(
        functools.partial(main_kernel, D, R),
        out_shape=(
            jax.ShapeDtypeStruct((F, N), BF16),
            jax.ShapeDtypeStruct((F, N), F32),
            jax.ShapeDtypeStruct((D, K, F, T), BF16),
            jax.ShapeDtypeStruct((G, D, rows, 4 * F), F32),
        ),
        in_specs=[vmem, vmem, vmem, smem, smem, smem, hbm, hbm, hbm],
        out_specs=(vmem, vmem, vmem, vmem),
        scratch_shapes=[
            pltpu.VMEM((B, L, T, T), BF16),
            pltpu.VMEM((D, K, T, T), BF16),
            pltpu.VMEM((F, N), BF16),
            pltpu.VMEM((B, F, T), BF16),
            pltpu.VMEM((D, K, F, T), BF16),
            pltpu.VMEM((D, K, F, T), BF16),
            pltpu.VMEM((B, F + KEEP, T), F32),
            pltpu.VMEM((D * K, F + KEEP, T), F32),
            pltpu.VMEM((KEEP, N), F32),
            pltpu.VMEM((R, F, 2 * F), BF16),
            pltpu.VMEM((R, F, 2 * F), BF16),
            pltpu.VMEM((2, 2, F, R * F), BF16),
            pltpu.VMEM((2, F, N), BF16),
            pltpu.VMEM((CHUNKS, 2, F, CH), BF16),
            pltpu.VMEM((CHUNKS, F, CH), F32),
            pltpu.VMEM((G, CHUNKS, F, CH), BF16),
            pltpu.VMEM((G, CHUNKS, F, CH), BF16),
            pltpu.VMEM((CHUNKS, R, F, CH), BF16),
            pltpu.VMEM((D, G, rows, 4 * F), F32),
            pltpu.VMEM((D, G, rows, 4 * F), F32),
            pltpu.VMEM((G, rows, 4 * F), F32),
            pltpu.VMEM((B, F, T), BF16),
            pltpu.VMEM((D, K, F, T), BF16),
            pltpu.VMEM((L, B // CHUNKS, F, T), F32),
            dma((3,)),
            dma((D,)),
            dma((D,)),
            dma((R,)),
            dma((R,)),
            dma((R,)),
            dma((R,)),
            dma,
            dma,
            dma((CHUNKS,)),
            dma((CHUNKS,)),
            dma((G, CHUNKS)),
            dma((G, CHUNKS)),
            dma((G, CHUNKS)),
            dma((G, CHUNKS)),
            dma((G, CHUNKS)),
            dma((G, CHUNKS)),
            dma((D,)),
            dma((D,)),
            dma((D,)),
            dma((D,)),
            dma((G, D)),
            dma((G, D)),
        ],
        compiler_params=pltpu.CompilerParams(
            collective_id=0, has_side_effects=True, vmem_limit_bytes=limit
        ),
        name="layer_main",
    )(
        feats,
        w_self.T,
        w_neigh.T,
        local_cols.T,
        slist,
        rrows,
        local_tiles,
        far_tiles,
        cotangent,
    )
    output, grad_feats, gs, gn = pl.pallas_call(
        finish_kernel,
        out_shape=(
            jax.ShapeDtypeStruct((F, N), BF16),
            jax.ShapeDtypeStruct((F, N), BF16),
            jax.ShapeDtypeStruct((F, R * F), F32),
            jax.ShapeDtypeStruct((F, R * F), F32),
        ),
        in_specs=[smem, hbm, hbm, hbm, hbm],
        out_specs=(vmem, vmem, vmem, vmem),
        scratch_shapes=[
            pltpu.VMEM((F, N), F32),
            pltpu.VMEM((D, K, F, T), BF16),
            pltpu.VMEM((G, D, rows, 4 * F), F32),
            dma((4,)),
        ],
        compiler_params=pltpu.CompilerParams(vmem_limit_bytes=limit),
        name="finish",
    )(slist, acc, back, final, output)
    return output, grad_feats, gs.T, gn.T


def solution(mesh):
    placed = (
        P("rep", "dom"),
        P(None, "rep"),
        P(None, "rep"),
        P("dom", None),
        P("dom", None, None, None),
        P("dom", None, None),
        P("dom", None, None),
        P("dom", None, None, None, None),
        P("rep", "dom"),
    )
    return jax.shard_map(
        functools.partial(local, mesh.shape["dom"], mesh.shape["rep"]),
        mesh=mesh,
        in_specs=placed,
        out_specs=(P("rep", "dom"), P("rep", "dom"), P(None, "rep"), P(None, "rep")),
        check_vma=False,
    )
```

```python
import functools

import jax
import jax.numpy as jnp
from jax import lax
from jax.experimental import pallas as pl
from jax.experimental.pallas import tpu as pltpu
from jax.sharding import PartitionSpec as P

MESH = pl.DeviceIdType.MESH
F32 = jnp.float32
BF16 = jnp.bfloat16
CHUNKS = 4
ONES = 16
KEEP = 8
NT = (((1,), (1,)), ((), ()))


def mm(a, b):
    return jnp.dot(a, b, preferred_element_type=F32)


def mm_nt(a, b):
    return lax.dot_general(a, b, NT, preferred_element_type=F32)


def equal_one(x, y):
    gap = x - y
    return (1 - jnp.minimum(gap * gap, 1)).astype(F32)


def rcopy(src, dst, send, recv, dom, rep):
    return pltpu.make_async_remote_copy(
        src_ref=src,
        dst_ref=dst,
        send_sem=send,
        recv_sem=recv,
        device_id={"dom": dom, "rep": rep},
        device_id_type=MESH,
    )


def greet(devices):
    barrier = pltpu.get_barrier_semaphore()
    for dom, rep in devices:
        pl.semaphore_signal(
            barrier, inc=1, device_id={"dom": dom, "rep": rep}, device_id_type=MESH
        )
    pl.semaphore_wait(barrier, len(devices))


def main_kernel(
    D,
    R,
    feats,
    wts_in,
    wtn_in,
    cols,
    slist,
    rrows,
    ltiles_h,
    rtiles_h,
    cot_h,
    out_o,
    acc_o,
    back_o,
    final_o,
    ltiles,
    rtiles,
    cot,
    blocks_of,
    hsend,
    hrecv,
    summed,
    far,
    inv,
    wts,
    wtn,
    wb,
    xf,
    xa,
    own,
    psend,
    precv,
    gp,
    gw,
    gpart,
    red,
    scaled,
    ret,
    nearb,
    loc_sem,
    h_s,
    h_r,
    ws_s,
    ws_r,
    wn_s,
    wn_r,
    xf_s,
    xf_r,
    xa_s,
    xa_r,
    pp_s,
    pp_r,
    gx_s,
    gx_r,
    gc_s,
    gc_r,
    b_s,
    b_r,
    p_s,
    p_r,
    f_s,
    f_r,
):
    d, r = lax.axis_index("dom"), lax.axis_index("rep")
    G = R // 2
    c, g = lax.rem(r, 2), lax.div(r, 2)
    mate = g * 2 + 1 - c
    F, N = feats.shape
    B, L, T, _ = ltiles.shape
    K = slist.shape[0]
    CH = N // CHUNKS
    CB = B // CHUNKS

    def cross(q):
        return lax.rem(g + q, G) * 2 + c

    loads = [
        pltpu.make_async_copy(ltiles_h, ltiles, loc_sem.at[0]),
        pltpu.make_async_copy(rtiles_h, rtiles, loc_sem.at[1]),
        pltpu.make_async_copy(cot_h, cot, loc_sem.at[2]),
    ]
    for load in loads:
        load.start()
    for b in range(B):
        blocks_of[b] = feats[:, b * T : (b + 1) * T]
    greet(
        [
            (lax.rem(d + p, D), cross(q))
            for q in range(G)
            for p in range(D)
            if p or q
        ]
        + [(d, lax.rem(g + q, G) * 2 + 1 - c) for q in range(G)]
    )

    def halo(p):
        return rcopy(
            hsend.at[p], hrecv.at[p], h_s.at[p], h_r.at[p], lax.rem(d + p, D), r
        )

    def pick(p, dst):
        for k in range(K):
            dst[p, k] = blocks_of[slist[k, lax.rem(d + p, D)]]

    def send_halo(p, carry):
        pick(p, hsend)
        halo(p).start()
        return carry

    lax.fori_loop(1, D, send_halo, 0)
    pick(0, hrecv)
    weight_copies, cross_weights = [], []
    sets = ((wts_in, wts, ws_s, ws_r), (wtn_in, wtn, wn_s, wn_r))
    chip = pl.ds(pl.multiple_of(g * 2 * F, 2 * F), 2 * F)
    for q in range(1, G):
        there = lax.rem(g + q, G)
        cut = pl.ds(pl.multiple_of(there * 2 * F, 2 * F), 2 * F)
        for src, dst, ss, rs in sets:
            cross_weights.append(
                rcopy(src.at[:, cut], dst.at[r], ss.at[q], rs.at[q], d, cross(q))
            )
    for src, dst, ss, rs in sets:
        weight_copies.append(
            rcopy(src.at[:, chip], dst.at[r], ss.at[0], rs.at[0], d, mate)
        )
    for copy in cross_weights + weight_copies:
        copy.start()
    feat_copy = rcopy(feats, xf.at[c], xf_s, xf_r, d, mate)
    feat_copy.start()
    wts[r] = wts_in[:, chip]
    wtn[r] = wtn_in[:, chip]
    xf[c] = feats[...]

    ones = jnp.ones((ONES, T), BF16)
    ones_wide = jnp.ones((ONES, L * T), BF16)
    loads[0].wait()

    def near(b, carry):
        left = jnp.concatenate(
            [
                blocks_of[cols[l, b]]
                for l in range(L)
            ],
            axis=1,
        )
        left = jnp.concatenate([left, ones_wide], axis=0)
        right = jnp.concatenate([ltiles[b, l] for l in range(L)], axis=1)
        summed[b] = mm_nt(left, right)[: F + KEEP]
        return carry

    lax.fori_loop(0, B, near, 0, unroll=4)
    for copy in cross_weights:
        copy.wait_recv()
    for q in range(1, G):
        t = lax.rem(g - q + G, G) * 2 + c
        for _, dst, ss, rs in sets:
            slot = G + q - 1
            copy = rcopy(dst.at[t], dst.at[t], ss.at[slot], rs.at[slot], d, mate)
            copy.start()
            weight_copies.append(copy)
    loads[1].wait()

    def far_step(p, carry):
        source = lax.rem(d - p + D, D)
        for k in range(K):
            left = jnp.concatenate([hrecv[p, k], ones], axis=0)
            far[p * K + k] = mm_nt(left, rtiles[source, k])[: F + KEEP]
        return carry

    def far_wait(p, carry):
        halo(p).wait_recv()
        return carry

    far_step(0, 0)
    lax.fori_loop(1, D, far_wait, 0)
    lax.fori_loop(1, D, far_step, 0, unroll=7)

    agg_copies = []
    for ch in range(CHUNKS):

        def place(i, carry):
            b = ch * CB + i
            total = summed[b]

            def add(p, total):
                source = lax.rem(d - p + D, D)
                for k in range(K):
                    hit = equal_one(rrows[k, source], b)
                    total = total + far[p * K + k] * hit
                return total

            total = lax.fori_loop(0, D, add, total, unroll=8)
            inverse = 1.0 / (1.0 + total[F:])
            at = pl.multiple_of(i * T, T)
            whole_at = pl.multiple_of(b * T, T)
            inv[:, pl.ds(whole_at, T)] = inverse
            xa[ch, c, :, pl.ds(at, T)] = (total[:F] * inverse[:1]).astype(BF16)
            return carry

        lax.fori_loop(0, CB, place, 0)
        copy = rcopy(xa.at[ch, c], xa.at[ch, c], xa_s.at[ch], xa_r.at[ch], d, mate)
        copy.start()
        agg_copies.append(copy)

    for copy in weight_copies:
        copy.wait_recv()
    for i, ref in enumerate((wts, wtn)):
        block = ref[...].reshape(R * F, 2 * F)
        turned = block.astype(F32).T.astype(BF16)
        wb[i] = turned.reshape(2, F, R * F)
    lefts = []
    for q in range(G):
        t = cross(q)
        lefts.append(jnp.concatenate([wts[t], wtn[t]], axis=1))
    left = jnp.concatenate(lefts, axis=0)
    feat_copy.wait_recv()

    def stacked(ch):
        near_part = xf[:, :, ch * CH : (ch + 1) * CH].reshape(2 * F, CH)
        return jnp.concatenate([near_part, xa[ch].reshape(2 * F, CH)], axis=0)

    part_copies = []
    for ch in range(CHUNKS):
        agg_copies[ch].wait_recv()
        part = mm(left, stacked(ch))
        for q in range(1, G):
            psend[q, ch] = part[q * F : (q + 1) * F].astype(BF16)
            copy = rcopy(
                psend.at[q, ch],
                precv.at[q, ch],
                pp_s.at[q, ch],
                pp_r.at[q, ch],
                d,
                cross(q),
            )
            copy.start()
            part_copies.append(copy)
        own[ch] = part[:F]

    loads[2].wait()
    cross_copies, mate_copies = [], []
    for ch in range(CHUNKS):
        preact = own[ch]
        for q in range(1, G):
            part_copies[ch * (G - 1) + q - 1].wait_recv()
            preact = preact + precv[q, ch].astype(F32)
        s = jax.nn.sigmoid(preact)
        at = slice(ch * CH, (ch + 1) * CH)
        out_o[:, at] = (preact * s).astype(BF16)
        slope = s * (1.0 + preact * (1.0 - s))
        gp[ch, r] = (cot[:, at].astype(F32) * slope).astype(BF16)
        for q in range(1, G):
            copy = rcopy(
                gp.at[ch, r],
                gp.at[ch, r],
                gx_s.at[q, ch],
                gx_r.at[q, ch],
                d,
                cross(q),
            )
            copy.start()
            cross_copies.append(copy)
        copy = rcopy(
            gp.at[ch, r], gp.at[ch, r], gc_s.at[0, ch], gc_r.at[0, ch], d, mate
        )
        copy.start()
        mate_copies.append(copy)

    back_left = jnp.concatenate([wb[0, c], wb[1, c]], axis=0)

    def back_chunk(ch):
        later = CHUNKS + ch * (G - 1)
        for copy in [mate_copies[ch]] + mate_copies[later : later + G - 1]:
            copy.wait_recv()
        back = mm(back_left, gp[ch].reshape(R * F, CH))
        for i in range(CB):
            b = ch * CB + i
            at = slice(i * T, (i + 1) * T)
            whole_at = slice(b * T, (b + 1) * T)
            acc_o[:, whole_at] = back[:F, at]
            scaled[b] = (back[F:, at] * inv[:1, whole_at]).astype(BF16)

    def scatter_all():
        def near_back(b, carry):
            right = jnp.concatenate([ltiles[b, l] for l in range(L)], axis=1)
            both = mm(scaled[b], right)
            for l in range(L):
                nearb[l, b] = both[:, l * T : (l + 1) * T]
            return carry

        lax.fori_loop(0, B, near_back, 0, unroll=4)

        def gather_back(block, carry):
            at = pl.ds(pl.multiple_of(block * T, T), T)

            def add(i, total):
                for l in range(L):
                    total = total + nearb[l, i] * equal_one(cols[l, i], block)
                return total

            acc_o[:, at] = lax.fori_loop(0, B, add, acc_o[:, at], unroll=8)
            return carry

        lax.fori_loop(0, B, gather_back, 0)

    grads = jnp.zeros((G * F, 4 * F), F32)
    for ch in range(CHUNKS):
        blocks = [gp[ch, r]]
        for q in range(1, G):
            cross_copies[ch * (G - 1) + q - 1].wait_recv()
            t = lax.rem(g - q + G, G) * 2 + c
            copy = rcopy(
                gp.at[ch, t], gp.at[ch, t], gc_s.at[q, ch], gc_r.at[q, ch], d, mate
            )
            copy.start()
            mate_copies.append(copy)
        for q in range(1, G):
            blocks.append(gp[ch, cross(q)])
        grads = grads + mm_nt(jnp.concatenate(blocks, axis=0), stacked(ch))
        if ch >= 1:
            back_chunk(ch - 1)
    rows = gw.shape[2]
    for p in range(D):
        for q in range(G):
            gw[p, q] = grads[q * F + p * rows : q * F + (p + 1) * rows]

    def piece(p):
        to = lax.rem(d + p, D)
        return rcopy(gw.at[to], gpart.at[p], p_s.at[p], p_r.at[p], to, r)

    def send_piece(p, carry):
        piece(p).start()
        return carry

    lax.fori_loop(1, D, send_piece, 0)

    back_chunk(CHUNKS - 1)

    def away(p, dst, slot):
        source = lax.rem(d + p, D)
        for k in range(K):
            block = scaled[rrows[k, source]]
            dst[slot, k] = mm(block, rtiles[source, k]).astype(BF16)

    def returned(p):
        to = lax.rem(d + p, D)
        return rcopy(ret.at[p], back_o.at[d], b_s.at[p], b_r.at[p], to, r)

    def send_back(p, carry):
        away(p, ret, p)
        returned(p).start()
        return carry

    lax.fori_loop(1, D, send_back, 0, unroll=7)
    away(0, back_o, d)

    def take_piece(p, total):
        piece(p).wait_recv()
        return total + gpart[p]

    red[...] = lax.fori_loop(1, D, take_piece, gw[d])
    finals = []
    for q in range(G):
        for p in range(D):
            if p or q:
                copy = rcopy(
                    red.at[q],
                    final_o.at[g, d],
                    f_s.at[q, p],
                    f_r.at[q, p],
                    lax.rem(d + p, D),
                    cross(q),
                )
                copy.start()
                finals.append(copy)
    final_o[g, d] = red[0]

    scatter_all()

    def finish_back(p, carry):
        returned(p).wait()
        piece(p).wait_send()
        return carry

    lax.fori_loop(1, D, finish_back, 0)
    for copy in finals:
        copy.wait_recv()

    def drain(p, carry):
        halo(p).wait_send()
        return carry

    lax.fori_loop(1, D, drain, 0)
    for copy in (
        weight_copies
        + cross_weights
        + [feat_copy]
        + agg_copies
        + part_copies
        + cross_copies
        + mate_copies
        + finals
    ):
        copy.wait_send()


def finish_kernel(
    slist, acc_h, back_h, final_h, out_h, out_o, gf_o, gs_o, gn_o, total, back, final, sem
):
    F, N = acc_h.shape
    loads = [
        pltpu.make_async_copy(src, dst, sem.at[i])
        for i, (src, dst) in enumerate(
            ((out_h, out_o), (acc_h, total), (back_h, back), (final_h, final))
        )
    ]
    for load in loads:
        load.start()
    D, K, _, T = back.shape
    G, _, rows, width = final.shape
    half = width // 2
    for load in loads[1:]:
        load.wait()

    def home(s, carry):
        for k in range(K):
            at = pl.ds(pl.multiple_of(slist[k, s] * T, T), T)
            total[:, at] = total[:, at] + back[s, k].astype(F32)
        return carry

    lax.fori_loop(0, D, home, 0)
    gf_o[...] = total[...].astype(BF16)
    for h in range(G):
        at = slice(h * half, (h + 1) * half)
        for p in range(D):
            part = final[h, p]
            where = slice(p * rows, (p + 1) * rows)
            gs_o[where, at] = part[:, :half]
            gn_o[where, at] = part[:, half:]
    loads[0].wait()


def local(
    D,
    R,
    feats,
    w_self,
    w_neigh,
    local_cols,
    local_tiles,
    send_list,
    remote_rows,
    remote_tiles,
    cotangent,
):
    F, N = feats.shape
    B, L, T, _ = local_tiles.shape
    K = send_list.shape[2]
    G = R // 2
    CH = N // CHUNKS
    rows = F // D
    vmem = pl.BlockSpec(memory_space=pltpu.VMEM)
    smem = pl.BlockSpec(memory_space=pltpu.SMEM)
    hbm = pl.BlockSpec(memory_space=pl.ANY)
    dma = pltpu.SemaphoreType.DMA
    slist = jnp.swapaxes(send_list, 1, 2)[0]
    rrows = jnp.swapaxes(remote_rows, 1, 2)[0]
    far_tiles = remote_tiles[0]
    limit = 60 * 1024 * 1024
    output, acc, back, final = pl.pallas_call(
        functools.partial(main_kernel, D, R),
        out_shape=(
            jax.ShapeDtypeStruct((F, N), BF16),
            jax.ShapeDtypeStruct((F, N), F32),
            jax.ShapeDtypeStruct((D, K, F, T), BF16),
            jax.ShapeDtypeStruct((G, D, rows, 4 * F), F32),
        ),
        in_specs=[vmem, vmem, vmem, smem, smem, smem, hbm, hbm, hbm],
        out_specs=(vmem, vmem, vmem, vmem),
        scratch_shapes=[
            pltpu.VMEM((B, L, T, T), BF16),
            pltpu.VMEM((D, K, T, T), BF16),
            pltpu.VMEM((F, N), BF16),
            pltpu.VMEM((B, F, T), BF16),
            pltpu.VMEM((D, K, F, T), BF16),
            pltpu.VMEM((D, K, F, T), BF16),
            pltpu.VMEM((B, F + KEEP, T), F32),
            pltpu.VMEM((D * K, F + KEEP, T), F32),
            pltpu.VMEM((KEEP, N), F32),
            pltpu.VMEM((R, F, 2 * F), BF16),
            pltpu.VMEM((R, F, 2 * F), BF16),
            pltpu.VMEM((2, 2, F, R * F), BF16),
            pltpu.VMEM((2, F, N), BF16),
            pltpu.VMEM((CHUNKS, 2, F, CH), BF16),
            pltpu.VMEM((CHUNKS, F, CH), F32),
            pltpu.VMEM((G, CHUNKS, F, CH), BF16),
            pltpu.VMEM((G, CHUNKS, F, CH), BF16),
            pltpu.VMEM((CHUNKS, R, F, CH), BF16),
            pltpu.VMEM((D, G, rows, 4 * F), F32),
            pltpu.VMEM((D, G, rows, 4 * F), F32),
            pltpu.VMEM((G, rows, 4 * F), F32),
            pltpu.VMEM((B, F, T), BF16),
            pltpu.VMEM((D, K, F, T), BF16),
            pltpu.VMEM((L, B, F, T), F32),
            dma((3,)),
            dma((D,)),
            dma((D,)),
            dma((R,)),
            dma((R,)),
            dma((R,)),
            dma((R,)),
            dma,
            dma,
            dma((CHUNKS,)),
            dma((CHUNKS,)),
            dma((G, CHUNKS)),
            dma((G, CHUNKS)),
            dma((G, CHUNKS)),
            dma((G, CHUNKS)),
            dma((G, CHUNKS)),
            dma((G, CHUNKS)),
            dma((D,)),
            dma((D,)),
            dma((D,)),
            dma((D,)),
            dma((G, D)),
            dma((G, D)),
        ],
        compiler_params=pltpu.CompilerParams(
            collective_id=0, has_side_effects=True, vmem_limit_bytes=limit
        ),
        name="layer_main",
    )(
        feats,
        w_self.T,
        w_neigh.T,
        local_cols.T,
        slist,
        rrows,
        local_tiles,
        far_tiles,
        cotangent,
    )
    output, grad_feats, gs, gn = pl.pallas_call(
        finish_kernel,
        out_shape=(
            jax.ShapeDtypeStruct((F, N), BF16),
            jax.ShapeDtypeStruct((F, N), BF16),
            jax.ShapeDtypeStruct((F, R * F), F32),
            jax.ShapeDtypeStruct((F, R * F), F32),
        ),
        in_specs=[smem, hbm, hbm, hbm, hbm],
        out_specs=(vmem, vmem, vmem, vmem),
        scratch_shapes=[
            pltpu.VMEM((F, N), F32),
            pltpu.VMEM((D, K, F, T), BF16),
            pltpu.VMEM((G, D, rows, 4 * F), F32),
            dma((4,)),
        ],
        compiler_params=pltpu.CompilerParams(vmem_limit_bytes=limit),
        name="finish",
    )(slist, acc, back, final, output)
    return output, grad_feats, gs.T, gn.T


def solution(mesh):
    placed = (
        P("rep", "dom"),
        P(None, "rep"),
        P(None, "rep"),
        P("dom", None),
        P("dom", None, None, None),
        P("dom", None, None),
        P("dom", None, None),
        P("dom", None, None, None, None),
        P("rep", "dom"),
    )
    return jax.shard_map(
        functools.partial(local, mesh.shape["dom"], mesh.shape["rep"]),
        mesh=mesh,
        in_specs=placed,
        out_specs=(P("rep", "dom"), P("rep", "dom"), P(None, "rep"), P(None, "rep")),
        check_vma=False,
    )
```
